32 devices in a mesh: seq: 8 (over y, x, core), head: 4 (over z).
Axes of the slice: x: 2, y: 2, z: 4, core: 2. Of those that a mesh axis runs over, the one named last changes fastest.
Arguments:
- query: bfloat16 [2048, 4096], P('seq', 'head'), may hold values from -6 to 6
- key: bfloat16 [2048, 4096], P('seq', 'head'), may hold values from -6 to 6
- value: bfloat16 [2048, 4096], P('seq', 'head'), may hold values from -6 to 6
- head_gain: float32 [4096], P('head'), may hold values from 0.1 to 1.9
- out_weight: bfloat16 [4096, 4096], P('head', 'seq'), may hold values from -0.09375 to 0.09375
- stream: bfloat16 [2048, 4096], P(('seq', 'head')), may hold values from -6 to 6
- model_gain: float32 [4096], replicated, may hold values from 0.1 to 1.9
- expert_ids: int32 [2048, 8], P(('seq', 'head')), may hold values from 0 to 31, all different within a row; in each aligned block of 64 rows (0 to 63, 64 to 127, ...) at most 24 rows name the same one
- expert_gates: float32 [2048, 8], P(('seq', 'head')), may hold values from 0.1 to 0.5
- gate_weight: bfloat16 [32, 4096, 768], P(('seq', 'head')), may hold values from -0.09375 to 0.09375
- up_weight: bfloat16 [32, 4096, 768], P(('seq', 'head')), may hold values from -0.09375 to 0.09375
- down_weight: bfloat16 [32, 768, 4096], P(('seq', 'head')), may hold values from -0.21875 to 0.21875
- weight_scales: float32 [32, 3], P(('seq', 'head')), may hold values from 0.6 to 1.6
Outputs:
- layer_out: bfloat16 [2048, 4096], P(('seq', 'head'))
The draws below stay inside these ranges and needn't reach their ends.
Inputs may be any that keep to these rules, and one draw needn't show every extreme that they name: `expert_ids`: among the 64 tokens of one device (aligned blocks of rows), no expert is named more than 24 times, a bound that some block reaches; the entries of one row differ.
All inputs are finite; a program needn't handle non-finite values.
Results may differ from the reference program's by a relative error of at most 0.013.
Values may be sent and summed in bfloat16 or wider, within the bound.
A program may use at most 128 MiB of HBM per device.

```python
import math
import jax
import jax.numpy as jnp
import numpy as np
from jax import lax

D = 4096
HEADS = 32
HD = 128
FF = 768
TOPK = 8
SEQ_DEV = 256
TOK_DEV = 64
EXPERTS = 32
CAP = 24
TOKENS = 2048
N_SEQ = 8
N_HEAD = 4


def shard_levels(rng, dims, split, smallest, top_value):
    factor_of, own = 1.0, jax.random.fold_in(rng, 6)
    for axis_at, parts in split:
        heights = jnp.exp(jax.random.uniform(jax.random.fold_in(own, axis_at), (parts,), jnp.float32, smallest / len(split), top_value / len(split)))
        factor_of = factor_of * jnp.repeat(heights, dims[axis_at] // parts).reshape([-1 if axis == axis_at else 1 for axis in range(len(dims))])
    return factor_of


def shared_out(rng, own, number, rows, count, top, bound, lean):
    order = jax.random.permutation(rng, count)
    packed, usual = shares(count, rows * top, bound, lean, True), shares(count, rows * top, bound, lean, False)
    places = jnp.arange(count)

    def named(tallies, rotation):
        used = int((tallies > 0).sum())
        fixed = max(1, used // 4)
        passed = fixed + (places - fixed + rotation * (used - fixed)) % max(1, count - fixed)
        return jnp.zeros((count,), jnp.int32).at[order[jnp.where(places < fixed, places, passed)]].set(jnp.asarray(tallies, jnp.int32))

    tallies = jnp.where(number % 4 == 0, named(packed, number // 4), named(usual, number - number // 4 - 1))
    mixed = jax.random.permutation(jax.random.fold_in(own, 3), count)
    donor, receiver = mixed[0:count // 2 * 2:2], mixed[1:count // 2 * 2:2]
    margin = jnp.minimum(tallies[donor] - 1, bound - tallies[receiver]) // 2
    margin = jnp.where((donor == order[0]) | (receiver == order[0]) | (tallies[receiver] == 0), 0, jnp.maximum(margin, 0))
    passed = jax.random.randint(jax.random.fold_in(own, 4), (count // 2,), 0, 1 << 20) % (margin + 1)
    tallies = tallies.at[donor].add(-passed).at[receiver].add(passed)
    members = jnp.searchsorted(jnp.cumsum(tallies), jnp.arange(rows * top), side="right").astype(jnp.int32)
    listing = members.reshape(top, rows).T
    listing = listing[jax.random.permutation(jax.random.fold_in(own, 1), rows)]
    rotation = jax.random.randint(jax.random.fold_in(own, 2), (rows, 1), 0, top)
    return jnp.take_along_axis(listing, (jnp.arange(top)[None, :] + rotation) % top, axis=1)


def shares(count, total, most, lean, full):
    portions = [(1 << 20) // math.isqrt(standing ** lean) + 1 for standing in range(1, count + 1)]
    largest = most if full else min(most, max(-(-total // count), total * portions[0] // sum(portions)))
    least = 1 if total - largest >= count - 1 else 0
    given, spare = [largest] + [least] * (count - 1), total - largest - least * (count - 1)
    while spare > 0:
        candidates = [i for i in range(1, count) if given[i] < largest] or [i for i in range(1, count) if given[i] < most]
        mass, remaining = sum([portions[i] for i in candidates]), spare
        for i in candidates:
            more = min(most - given[i], max(1, remaining * portions[i] // mass), spare)
            given[i] = given[i] + more
            spare = spare - more
    return np.array(given)


def normal_values(key, shape, width, reach, pieces=(), kind=jnp.bfloat16):
    result = jax.random.normal(key, shape, jnp.float32) * width
    if len(pieces) > 0:
        result = shard_levels(key, shape, pieces, -0.22, 0.18) * result
    return jnp.clip(result, min=-reach, max=reach).astype(kind)


def setup_inputs(seed: int = 0) -> dict:
    key_list = jax.random.split(jax.random.key(seed), 14)
    query = normal_values(key_list[0], (TOKENS, HEADS * HD), 1.0, 6.0, ((0, 8), (1, 4)))
    key = normal_values(key_list[1], (TOKENS, HEADS * HD), 1.0, 6.0, ((0, 8), (1, 4)))
    value = normal_values(key_list[2], (TOKENS, HEADS * HD), 1.0, 6.0, ((0, 8), (1, 4)))
    head_gain = jnp.clip(1.0 + 0.18 * jax.random.normal(key_list[3], (HEADS * HD,), jnp.float32), 0.1, 1.9)
    out_weight = normal_values(key_list[4], (HEADS * HD, D), (HEADS * HD) ** -0.5, 0.09375, ((0, 4), (1, 8)))
    stream = normal_values(key_list[5], (TOKENS, D), 1.0, 6.0, ((0, 32),))
    model_gain = jnp.clip(1.0 + 0.18 * jax.random.normal(key_list[6], (D,), jnp.float32), 0.1, 1.9)
    expert_ids_keys = jax.random.split(jax.random.fold_in(key_list[7], 1), TOKENS // TOK_DEV)
    expert_ids_turns = jax.random.permutation(jax.random.fold_in(key_list[7], 3), TOKENS // TOK_DEV)
    expert_ids = jax.vmap(lambda own, number: shared_out(jax.random.fold_in(key_list[7], 2), own, number, TOK_DEV, EXPERTS, TOPK, CAP, 2))(expert_ids_keys, expert_ids_turns).reshape((TOKENS, TOPK))
    expert_gates = jnp.clip(0.1 + 0.4 * jax.random.uniform(key_list[8], (TOKENS, TOPK), jnp.float32) ** shard_levels(key_list[8], (TOKENS, TOPK), ((0, 32),), -0.2, 0.2), 0.1, 0.5)
    gate_weight = normal_values(key_list[9], (EXPERTS, D, FF), D ** -0.5, 0.09375, ((0, 32),))
    up_weight = normal_values(key_list[10], (EXPERTS, D, FF), D ** -0.5, 0.09375, ((0, 32),))
    down_weight = normal_values(key_list[11], (EXPERTS, FF, D), FF ** -0.5, 0.21875, ((0, 32),))
    weight_scales = jnp.clip(jnp.exp(math.log(1.6) - 0.98082923 * jax.random.uniform(key_list[12], (EXPERTS, 3), jnp.float32) ** shard_levels(key_list[12], (EXPERTS, 3), ((0, 32),), -0.2, 0.2)), 0.6, 1.6)
    return dict(query=query, key=key, value=value, head_gain=head_gain, out_weight=out_weight, stream=stream, model_gain=model_gain, expert_ids=expert_ids, expert_gates=expert_gates, gate_weight=gate_weight, up_weight=up_weight, down_weight=down_weight, weight_scales=weight_scales)


def to_bf16_value(array):
    return lax.optimization_barrier(array.astype(jnp.bfloat16)).astype(jnp.float32)

def reference(query, key, value, head_gain, out_weight, stream, model_gain, expert_ids, expert_gates, gate_weight, up_weight, down_weight, weight_scales):
    query_blocks = query.reshape(N_SEQ, SEQ_DEV, HEADS, HD)
    key_blocks = key.reshape(N_SEQ, SEQ_DEV, HEADS, HD)
    value_blocks = value.reshape(N_SEQ, SEQ_DEV, HEADS, HD)
    causal = jnp.tril(jnp.ones((SEQ_DEV, SEQ_DEV), dtype=bool))

    def block_step(carried, slices):
        query_rows, key_rows, value_rows = slices
        query_float = query_rows.astype(jnp.float32)
        key_float = key_rows.astype(jnp.float32)
        value_float = value_rows.astype(jnp.float32)
        scores = jnp.einsum('thd,shd->hts', query_float, key_float)
        scores = to_bf16_value(jnp.where(causal[None, :, :], scores, 0.0))
        local_part = jnp.einsum('hts,shd->thd', scores, value_float)
        prior_state = to_bf16_value(carried)
        earlier_part = jnp.einsum('thd,hde->the', query_float, prior_state)
        updated = carried + jnp.einsum('shd,she->hde', key_float, value_float)
        return (updated, local_part + earlier_part)
    initial = jnp.zeros((HEADS, HD, HD), jnp.float32)
    final_state, mixed_heads = lax.scan(block_step, initial, (query_blocks, key_blocks, value_blocks))
    mixed_heads = mixed_heads.reshape(TOKENS, HEADS, HD)
    mean_square = lax.optimization_barrier(jnp.mean(mixed_heads * mixed_heads, axis=-1, keepdims=True))
    head_normed = (mixed_heads * lax.rsqrt(mean_square + 1e-06) * head_gain.reshape(HEADS, HD)).astype(jnp.bfloat16)
    head_normed = head_normed.reshape(TOKENS, HEADS * HD)
    attention = jnp.dot(head_normed.astype(jnp.float32), out_weight.astype(jnp.float32))
    residual = (stream.astype(jnp.float32) + attention).astype(jnp.bfloat16)
    residual_float = residual.astype(jnp.float32)
    mean_square = lax.optimization_barrier(jnp.mean(residual_float * residual_float, axis=-1, keepdims=True))
    normed = (residual_float * lax.rsqrt(mean_square + 1e-06) * model_gain).astype(jnp.bfloat16)
    most_rows = CAP * N_SEQ * N_HEAD

    def expert_step(expert_mix, slices):
        expert, gate_matrix, up_matrix, down_matrix, scale_row = slices
        chosen = expert_ids == expert
        token_weight = lax.optimization_barrier(jnp.sum(jnp.where(chosen, expert_gates, 0.0), axis=1))
        has_expert = jnp.any(chosen, axis=1)
        row_index = jnp.nonzero(has_expert, size=most_rows, fill_value=0)[0].astype(jnp.int32)
        live_count = jnp.sum(has_expert.astype(jnp.int32))
        is_live = (jnp.arange(most_rows, dtype=jnp.int32) < live_count).astype(jnp.float32)
        inputs = normed[row_index].astype(jnp.float32)
        gate_part = jnp.dot(inputs, gate_matrix.astype(jnp.float32)) * scale_row[0]
        up_part = jnp.dot(inputs, up_matrix.astype(jnp.float32)) * scale_row[1]
        act = to_bf16_value(jax.nn.silu(gate_part) * up_part)
        expert_rows = to_bf16_value(jnp.dot(act, down_matrix.astype(jnp.float32)) * scale_row[2])
        weighted = expert_rows * (token_weight[row_index] * is_live)[:, None]
        return (expert_mix.at[row_index].add(weighted), None)
    expert_list = jnp.arange(EXPERTS, dtype=jnp.int32)
    expert_mix, unused = lax.scan(expert_step, jnp.zeros((TOKENS, D), jnp.float32), (expert_list, gate_weight, up_weight, down_weight, weight_scales))
    return (residual_float + expert_mix).astype(jnp.bfloat16)
```

```python
import functools

import jax
import jax.numpy as jnp
from jax import lax
from jax.experimental import pallas as pl
from jax.experimental.pallas import tpu as pltpu
from jax.sharding import PartitionSpec as P

HD = 128
SEG = 128
TOPK = 8
MESH = pl.DeviceIdType.MESH


def layer_kernel(
    seqs,
    heads,
    slots,
    q_hbm,
    k_hbm,
    v_hbm,
    gain_ref,
    w_hbm,
    stream_hbm,
    model_ref,
    ids_ref,
    gates_ref,
    scale_ref,
    gate_hbm,
    up_hbm,
    down_hbm,
    out_ref,
    q_ref,
    k_ref,
    v_ref,
    stream_ref,
    state,
    mixed,
    normed_heads,
    wbuf,
    tot,
    own,
    psend,
    precv,
    res,
    square,
    route_ids,
    route_gates,
    pick_ref,
    mix_ref,
    gate_v,
    up_v,
    gath,
    send,
    recv,
    back,
    rgath,
    rsend,
    rrecv,
    acc_g,
    acc_u,
    act,
    sds,
    sdr,
    sfs,
    sfr,
    wds,
    wdr,
    wfs,
    wfr,
    ids_s,
    ids_r,
    gts_s,
    gts_r,
    zs,
    zr,
    gs,
    gr,
    ps,
    pr,
    rs,
    rr,
    cs,
    cr,
    load_sem,
    wown_sem,
    wsem,
    dsem,
    osem,
    bsem,
):
    s = lax.axis_index("seq")
    h = lax.axis_index("head")
    tokens, features = q_ref.shape
    rows, width = stream_ref.shape
    hidden = gate_v.shape[1]
    local = features // HD
    block = w_hbm.shape[1]
    subs = block // SEG
    owners = seqs // 2
    chunks = 2 * subs
    step = owners * SEG
    halves = 2
    part = features // halves
    bits = [2**i for i in range(1, seqs.bit_length() - 1)]
    orders = [bits, bits[::-1]]
    evens = list(range(0, seqs, 2))
    far = sorted(range(1, seqs), key=lambda d: (-(d // 2).bit_count(), d))
    f32, bf = jnp.float32, jnp.bfloat16

    def flip(d):
        out, bit = s, 1
        while bit < seqs:
            if d & bit:
                out = out + bit * (1 - 2 * ((s // bit) % 2))
            bit *= 2
        return out

    partner = flip(1)

    def line(d):
        return lax.rem(h + d, heads)

    def cols(c):
        return pl.ds(pl.multiple_of(c * step, step), step)

    def seg(c, i):
        return pl.ds(pl.multiple_of(c * step + i * SEG, SEG), SEG)

    def home(c, i):
        at = (2 * i + c % 2) * block + (c // 2) * SEG
        return pl.ds(pl.multiple_of(at, SEG), SEG)

    def remote(src, dst, ssem, rsem, seq, head):
        return pltpu.make_async_remote_copy(
            src_ref=src,
            dst_ref=dst,
            send_sem=ssem,
            recv_sem=rsem,
            device_id=(seq, head),
            device_id_type=MESH,
        )

    def state_direct(slot, peer):
        return remote(state.at[slot], state.at[slot], sds.at[peer], sdr.at[slot], peer, h)

    def state_pass(slot):
        return remote(state.at[slot], state.at[slot], sfs.at[slot], sfr.at[slot], partner, h)

    def w_src(j, half):
        return w_hbm.at[pl.ds(half * part, part), pl.ds(pl.multiple_of(j * SEG, SEG), SEG)]

    def w_at(slot, j, half):
        return wbuf.at[
            2 * j + slot % 2,
            pl.ds(half * part, part),
            pl.ds(pl.multiple_of((slot // 2) * SEG, SEG), SEG),
        ]

    def w_first(j, half, bit):
        return remote(
            w_src(j, half), w_at(s, j, half),
            wds.at[s, j, half, bits.index(bit)], wdr.at[s, j, half], flip(bit), h,
        )

    def w_relay(slot, j, half, bit):
        return remote(
            w_at(slot, j, half), w_at(slot, j, half),
            wds.at[slot, j, half, bits.index(bit)], wdr.at[slot, j, half], flip(bit), h,
        )

    def later_bits(d, half):
        order = orders[half]
        last = max(order.index(bit) for bit in bits if d & bit)
        return order[last + 1 :]

    def w_pass(slot, j, half):
        return remote(
            w_at(slot, j, half), w_at(slot, j, half),
            wfs.at[slot, j, half], wfr.at[slot, j, half], partner, h,
        )

    def w_own_pass(j, half):
        return remote(
            w_src(j, half), w_at(s, j, half), wfs.at[s, j, half], wfr.at[s, j, half], partner, h
        )

    def w_own(j, half):
        return pltpu.make_async_copy(w_src(j, half), w_at(s, j, half), wown_sem.at[j, half])

    def w_start(j):
        for i in range(len(bits)):
            for half in range(halves):
                w_first(j, half, orders[half][i]).start()
        for half in range(halves):
            w_own_pass(j, half).start()

    def w_near(j):
        for half in range(halves):
            for d in evens:
                if d.bit_count() == 1:
                    w_relay(flip(d), j, half, bits[0]).wait_recv()
                    for bit in later_bits(d, half):
                        w_relay(flip(d), j, half, bit).start()
                    w_pass(flip(d), j, half).start()

    def w_far(j):
        for half in range(halves):
            for d in sorted(evens, key=lambda d: (d.bit_count(), d)):
                if d.bit_count() > 1:
                    w_relay(flip(d), j, half, bits[0]).wait_recv()
                    for bit in later_bits(d, half):
                        w_relay(flip(d), j, half, bit).start()
                    w_pass(flip(d), j, half).start()

    def w_passed(j):
        for half in range(halves):
            w_own(j, half).wait()
            for d in evens:
                w_pass(flip(d + 1), j, half).wait_recv()

    def w_drain(j):
        for half in range(halves):
            for bit in bits:
                w_first(j, half, bit).wait_send()
            w_own_pass(j, half).wait_send()
            for d in evens[1:]:
                for bit in later_bits(d, half):
                    w_relay(flip(d), j, half, bit).wait_send()
                w_pass(flip(d), j, half).wait_send()

    def ids_copy(slot, target):
        return remote(ids_ref, route_ids.at[slot], ids_s.at[target], ids_r.at[slot], s, target)

    def gates_copy(slot, target):
        return remote(
            gates_ref, route_gates.at[slot], gts_s.at[target], gts_r.at[slot], s, target
        )

    def weights(c, i):
        return (
            pltpu.make_async_copy(
                gate_hbm.at[0, home(c, i), :], gate_v.at[seg(c, i), :], wsem.at[0, c, i]
            ),
            pltpu.make_async_copy(
                up_hbm.at[0, home(c, i), :], up_v.at[seg(c, i), :], wsem.at[1, c, i]
            ),
        )

    def down_copy(c):
        return pltpu.make_async_copy(
            down_hbm.at[0, :, cols(c)], wbuf.at[c, pl.ds(0, hidden), :], dsem.at[c]
        )

    barrier = pltpu.get_barrier_semaphore()
    for d in range(1, seqs):
        pl.semaphore_signal(barrier, inc=1, device_id=(flip(d), h), device_id_type=MESH)
    for d in range(1, heads):
        pl.semaphore_signal(barrier, inc=1, device_id=(s, line(d)), device_id_type=MESH)
    loads = [
        pltpu.make_async_copy(source, target, load_sem.at[i])
        for i, (source, target) in enumerate(
            [(k_hbm, k_ref), (v_hbm, v_ref), (q_hbm, q_ref), (stream_hbm, stream_ref)]
        )
    ]
    for load in loads:
        load.start()

    def own_weights(j, carry):
        for half in range(halves):
            w_own(j, half).start()
        return carry

    lax.fori_loop(0, subs, own_weights, 0)
    route_ids[h] = ids_ref[...]
    route_gates[h] = gates_ref[...]
    loads[0].wait()
    loads[1].wait()

    def lanes(i):
        return pl.ds(pl.multiple_of(i * HD, HD), HD)

    def block_state(i, carry):
        total = lax.dot_general(
            k_ref[:, lanes(i)], v_ref[:, lanes(i)], (((0,), (0,)), ((), ())),
            preferred_element_type=f32,
        )
        state[s, i] = total.astype(bf)
        return carry

    lax.fori_loop(0, local, block_state, 0)
    pl.semaphore_wait(barrier, seqs + heads - 2)
    for d in range(2, seqs, 2):
        state_direct(s, flip(d)).start()
    state_pass(s).start()
    for d in range(1, heads):
        ids_copy(h, line(d)).start()
        gates_copy(h, line(d)).start()
    for j in range(min(2, subs)):
        w_start(j)

    def start_weights(c, carry):
        for i in range(owners):
            for copy in weights(c, i):
                copy.start()
        return carry

    lax.fori_loop(0, chunks, start_weights, 0)
    loads[2].wait()

    row = lax.broadcasted_iota(jnp.int32, (tokens, tokens), 0)
    col = lax.broadcasted_iota(jnp.int32, (tokens, tokens), 1)
    causal = col <= row

    def local_part(i, carry):
        scores = lax.dot_general(
            q_ref[:, lanes(i)], k_ref[:, lanes(i)], (((1,), (1,)), ((), ())),
            preferred_element_type=f32,
        )
        scores = jnp.where(causal, scores, 0.0).astype(bf)
        mixed[:, lanes(i)] = jnp.dot(scores, v_ref[:, lanes(i)], preferred_element_type=f32)
        return carry

    lax.fori_loop(0, local, local_part, 0)

    for d in range(1, heads):
        ids_copy(line(d), line(d)).wait_recv()
        gates_copy(line(d), line(d)).wait_recv()
    ids = route_ids[...].reshape(tokens, TOPK)
    gates = route_gates[...].reshape(tokens, TOPK)
    lane = lax.broadcasted_iota(jnp.int32, (tokens, 128), 1)
    hits = jnp.zeros((tokens, 128), f32)
    shares = jnp.zeros((tokens, 128), f32)
    for n in range(seqs):
        chosen = ids == n * heads + h
        hit = jnp.sum(jnp.where(chosen, 1.0, 0.0), axis=1, keepdims=True)
        share = jnp.sum(jnp.where(chosen, gates, 0.0), axis=1, keepdims=True)
        hits = jnp.where(lane == n, hit, hits)
        shares = jnp.where(lane == n, share, shares)
    earlier = jnp.where(col < row, 1.0, 0.0).astype(bf)
    rank = jnp.dot(earlier, hits.astype(bf), preferred_element_type=f32)
    place = jnp.where(hits > 0.5, rank, -1.0)
    spread_row = lax.broadcasted_iota(jnp.int32, (128, seqs * slots), 0)
    spread_col = lax.broadcasted_iota(jnp.int32, (128, seqs * slots), 1)
    inside = (spread_col >= spread_row * slots) & (spread_col < spread_row * slots + slots)
    spread = jnp.where(inside, 1.0, 0.0).astype(bf)
    slot_at = lax.broadcasted_iota(jnp.int32, (tokens, seqs * slots), 1)
    base = jnp.zeros((tokens, seqs * slots), jnp.int32)
    for n in range(1, seqs):
        base = jnp.where(slot_at >= n * slots, n * slots, base)
    slot_at = (slot_at - base).astype(f32)
    taken = jnp.dot(place.astype(bf), spread, preferred_element_type=f32) == slot_at
    shared = jnp.dot(shares.astype(bf), spread, preferred_element_type=f32)
    mix_ref[...] = jnp.where(taken, shared, 0.0).astype(bf)
    pick_ref[...] = jnp.where(taken, 1.0, 0.0).T.astype(bf)

    for d in range(2, seqs, 2):
        state_direct(flip(d), flip(d)).wait_recv()
        state_pass(flip(d)).start()
    for d in range(1, seqs, 2):
        state_pass(flip(d)).wait_recv()

    def earlier_part(i, carry):
        prior = jnp.zeros((HD, HD), f32)
        for c in range(seqs):
            prior = prior + jnp.where(c < s, state[c, i].astype(f32), 0.0)
        total = mixed[:, lanes(i)] + jnp.dot(
            q_ref[:, lanes(i)], prior.astype(bf), preferred_element_type=f32
        )
        mean_square = jnp.mean(total * total, axis=-1, keepdims=True)
        normed_heads[:, lanes(i)] = (
            total * lax.rsqrt(mean_square + 1e-06) * gain_ref[:, lanes(i)]
        ).astype(bf)
        return carry

    lax.fori_loop(0, local, earlier_part, 0)

    def sum_copy(sems, c, d):
        return remote(
            psend.at[line(d), :, cols(c)], precv.at[h, :, cols(c)],
            sems[0].at[c, d], sems[1].at[c, h], s, line(d),
        )

    def sum_arrival(sems, c, source):
        return remote(
            psend.at[source, :, cols(c)], precv.at[source, :, cols(c)],
            sems[0].at[c, 0], sems[1].at[c, source], s, source,
        )

    def gather_copy(c, d, source, target):
        at = gath.at[source, :, cols(c)]
        return remote(at, at, gs.at[c, d], gr.at[c, source], s, target)

    def rgather_copy(d, source, target):
        at = rgath.at[source]
        return remote(at, at, gs.at[chunks, d], gr.at[chunks, source], s, target)

    def plane_copy(c, d):
        return remote(
            send.at[flip(d), :, cols(c)], recv.at[s, :, cols(c)], ps.at[c, d], pr.at[c, s],
            flip(d), h,
        )

    def plane_arrival(c, source):
        return remote(
            send.at[source, :, cols(c)], recv.at[source, :, cols(c)], ps.at[c, 0],
            pr.at[c, source], source, h,
        )

    def own_copy(c):
        return pltpu.make_async_copy(
            send.at[s, :, cols(c)], recv.at[s, :, cols(c)], osem.at[c]
        )

    def rplane_copy(d):
        return remote(
            rsend.at[flip(d)], rrecv.at[s], ps.at[chunks, d], pr.at[chunks, s], flip(d), h
        )

    def rplane_arrival(source):
        return remote(
            rsend.at[source], rrecv.at[source], ps.at[chunks, 0], pr.at[chunks, source],
            source, h,
        )

    def rown_copy():
        return pltpu.make_async_copy(rsend.at[s], rrecv.at[s], osem.at[chunks])

    def split_heads(total, c, sems):
        tot[...] = total.reshape(heads, rows, step)
        own[:, cols(c)] = tot[h]
        psend[:, :, cols(c)] = tot[...].astype(bf)
        for d in range(1, heads):
            sum_copy(sems, c, d).start()

    def project(c):
        total = jnp.dot(
            normed_heads[...], wbuf[c, pl.ds(0, features), :], preferred_element_type=f32
        )
        split_heads(total, c, (zs, zr))

    def settle(c):
        for d in range(1, heads):
            sum_arrival((zs, zr), c, line(d)).wait_recv()
        for i in range(owners):
            total = own[:, seg(c, i)]
            for d in range(1, heads):
                total = total + precv[line(d), :, seg(c, i)].astype(f32)
            residual = (stream_ref[:, home(c, i)].astype(f32) + total).astype(bf)
            res[:, home(c, i)] = residual
            value = residual.astype(f32)
            square[...] += value * value
            gath[h, :, seg(c, i)] = (value * model_ref[:, home(c, i)]).astype(bf)
        for d in range(1, heads):
            gather_copy(c, d, h, line(d)).start()

    def settle_norm():
        mean_square = jnp.sum(square[...], axis=1, keepdims=True) / width
        factor = jnp.broadcast_to(lax.rsqrt(mean_square + 1e-06), (rows, 128))
        high = factor.astype(bf).astype(f32)
        low = (factor - high).astype(bf).astype(f32)
        at = lax.broadcasted_iota(jnp.int32, (rows, 128), 1)
        rgath[h] = jnp.where(at < 64, high, low).astype(bf)
        for d in range(1, heads):
            rgather_copy(d, h, line(d)).start()

    def dispatch(c):
        for d in range(1, heads):
            gather_copy(c, d, line(d), line(d)).wait_recv()
        picked = jnp.dot(
            pick_ref[...], gath[:, :, cols(c)].reshape(tokens, step),
            preferred_element_type=f32,
        )
        send[:, :, cols(c)] = picked.astype(bf).reshape(seqs, slots, step)
        for d in far:
            plane_copy(c, d).start()
        own_copy(c).start()

    def dispatch_norm():
        for d in range(1, heads):
            rgather_copy(d, line(d), line(d)).wait_recv()
        picked = jnp.dot(
            pick_ref[...], rgath[...].reshape(tokens, 128), preferred_element_type=f32
        )
        rsend[...] = picked.astype(bf).reshape(seqs, slots, 128)
        for d in far:
            rplane_copy(d).start()
        rown_copy().start()

    def expand(c):
        for i in range(owners):
            for copy in weights(c, i):
                copy.wait()
        for d in range(1, seqs):
            plane_arrival(c, flip(d)).wait_recv()
        own_copy(c).wait()
        lhs = recv[:, :, cols(c)].reshape(seqs * slots, step)
        acc_g[...] += jnp.dot(lhs, gate_v[cols(c), :], preferred_element_type=f32)
        acc_u[...] += jnp.dot(lhs, up_v[cols(c), :], preferred_element_type=f32)

    acc_g[...] = jnp.zeros_like(acc_g)
    acc_u[...] = jnp.zeros_like(acc_u)
    square[...] = jnp.zeros_like(square)
    loads[3].wait()

    w_near(0)
    if subs > 2:
        w_start(2)
    if subs > 1:
        w_near(1)
    w_far(0)
    w_passed(0)
    depth = 4

    def forward(t, carry):
        @pl.when(t < chunks)
        def _():
            project(t)

        @pl.when((t >= 1) & (t <= chunks))
        def _():
            settle(t - 1)

        @pl.when(t == chunks)
        def _():
            settle_norm()

        @pl.when((t >= 2) & (t <= chunks + 1))
        def _():
            dispatch(t - 2)

        @pl.when(t == chunks + 1)
        def _():
            dispatch_norm()

        @pl.when(t >= depth)
        def _():
            expand(t - depth)

        @pl.when(t + 3 < subs)
        def _():
            w_start(t + 3)

        @pl.when(t + 2 < subs)
        def _():
            w_near(t + 2)

        @pl.when(t + 1 < subs)
        def _():
            w_far(t + 1)
            w_passed(t + 1)

        return carry

    lax.fori_loop(0, chunks + depth, forward, 0)

    def release(j, carry):
        w_drain(j)
        return carry

    def start_down(c, carry):
        down_copy(c).start()
        return carry

    lax.fori_loop(0, subs, release, 0)
    lax.fori_loop(0, chunks, start_down, 0)

    for d in range(1, seqs):
        rplane_arrival(flip(d)).wait_recv()
    rown_copy().wait()
    gate_scale = scale_ref[0, 0]
    up_scale = scale_ref[0, 1]
    down_scale = scale_ref[0, 2]

    def activate(i, carry):
        at = pl.ds(pl.multiple_of(i * slots, slots), slots)
        factor = jnp.sum(rrecv[i].astype(f32), axis=1, keepdims=True) / 64
        g = acc_g[at, :] * (factor * gate_scale)
        u = acc_u[at, :] * (factor * up_scale)
        act[at, :] = (g / (1.0 + jnp.exp(-g)) * u).astype(bf)
        return carry

    lax.fori_loop(0, seqs, activate, 0)

    def back_copy(c, d):
        return remote(
            recv.at[flip(d), :, cols(c)], back.at[s, :, cols(c)], rs.at[c, d], rr.at[c, s],
            flip(d), h,
        )

    def back_arrival(c, source):
        return remote(
            recv.at[source, :, cols(c)], back.at[source, :, cols(c)], rs.at[c, 0],
            rr.at[c, source], source, h,
        )

    def own_back(c):
        return pltpu.make_async_copy(
            recv.at[s, :, cols(c)], back.at[s, :, cols(c)], bsem.at[c]
        )

    def contract(c, carry):
        down_copy(c).wait()
        rows_out = jnp.dot(
            act[...], wbuf[c, pl.ds(0, hidden), :], preferred_element_type=f32
        )
        recv[:, :, cols(c)] = (rows_out * down_scale).astype(bf).reshape(seqs, slots, step)
        for d in far:
            back_copy(c, d).start()
        own_back(c).start()
        for d in range(1, heads):
            sum_copy((zs, zr), c, d).wait_send()
        return carry

    lax.fori_loop(0, chunks, contract, 0)

    def combine(c):
        for d in range(1, seqs):
            back_arrival(c, flip(d)).wait_recv()
        own_back(c).wait()
        total = jnp.dot(
            mix_ref[...], back[:, :, cols(c)].reshape(seqs * slots, step),
            preferred_element_type=f32,
        )
        split_heads(total, c, (cs, cr))

    def finish(c):
        total = res[:, cols(c)].astype(f32) + own[:, cols(c)]
        for d in range(1, heads):
            sum_arrival((cs, cr), c, line(d)).wait_recv()
            total = total + precv[line(d), :, cols(c)].astype(f32)
        out_ref[:, cols(c)] = total.astype(bf)

    def backward(t, carry):
        @pl.when(t < chunks)
        def _():
            combine(t)

        @pl.when(t >= 1)
        def _():
            finish(t - 1)

        return carry

    lax.fori_loop(0, chunks + 1, backward, 0)

    for d in range(2, seqs, 2):
        state_direct(s, flip(d)).wait_send()
    for d in evens:
        state_pass(flip(d)).wait_send()
    for d in range(1, heads):
        ids_copy(h, line(d)).wait_send()
        gates_copy(h, line(d)).wait_send()
        rgather_copy(d, h, line(d)).wait_send()
    for d in range(1, seqs):
        rplane_copy(d).wait_send()

    def drain(c, carry):
        for d in range(1, heads):
            gather_copy(c, d, h, line(d)).wait_send()
            sum_copy((cs, cr), c, d).wait_send()
        for d in range(1, seqs):
            plane_copy(c, d).wait_send()
            back_copy(c, d).wait_send()
        return carry

    lax.fori_loop(0, chunks, drain, 0)


def body(
    query,
    key,
    value,
    head_gain,
    out_weight,
    stream,
    model_gain,
    expert_ids,
    expert_gates,
    gate_weight,
    up_weight,
    down_weight,
    weight_scales,
):
    seqs, heads = lax.axis_size("seq"), lax.axis_size("head")
    tokens, features = query.shape
    rows, width = stream.shape
    hidden = gate_weight.shape[2]
    local = features // HD
    block = out_weight.shape[1]
    subs = block // SEG
    owners = seqs // 2
    chunks = 2 * subs
    step = owners * SEG
    capacity = 3 * rows * TOPK // (2 * seqs * heads)
    slots = -(-capacity * heads // 16) * 16
    nbits = seqs.bit_length() - 2
    vmem = pl.BlockSpec(memory_space=pltpu.VMEM)
    smem = pl.BlockSpec(memory_space=pltpu.SMEM)
    anywhere = pl.BlockSpec(memory_space=pl.ANY)
    bf, f32 = jnp.bfloat16, jnp.float32
    dma = pltpu.SemaphoreType.DMA
    return pl.pallas_call(
        functools.partial(layer_kernel, seqs, heads, slots),
        out_shape=jax.ShapeDtypeStruct((rows, width), bf),
        in_specs=[anywhere] * 3 + [vmem] + [anywhere] * 2 + [vmem] * 3 + [smem] + [anywhere] * 3,
        out_specs=vmem,
        scratch_shapes=[
            pltpu.VMEM((tokens, features), bf),
            pltpu.VMEM((tokens, features), bf),
            pltpu.VMEM((tokens, features), bf),
            pltpu.VMEM((rows, width), bf),
            pltpu.VMEM((seqs, local, HD, HD), bf),
            pltpu.VMEM((tokens, features), f32),
            pltpu.VMEM((tokens, features), bf),
            pltpu.VMEM((chunks, max(features, hidden), step), bf),
            pltpu.VMEM((heads, rows, step), f32),
            pltpu.VMEM((rows, width), f32),
            pltpu.VMEM((heads, rows, width), bf),
            pltpu.VMEM((heads, rows, width), bf),
            pltpu.VMEM((rows, width), bf),
            pltpu.VMEM((rows, SEG), f32),
            pltpu.VMEM((heads, rows, TOPK), jnp.int32),
            pltpu.VMEM((heads, rows, TOPK), f32),
            pltpu.VMEM((seqs * slots, tokens), bf),
            pltpu.VMEM((tokens, seqs * slots), bf),
            pltpu.VMEM((width, hidden), bf),
            pltpu.VMEM((width, hidden), bf),
            pltpu.VMEM((heads, rows, width), bf),
            pltpu.VMEM((seqs, slots, width), bf),
            pltpu.VMEM((seqs, slots, width), bf),
            pltpu.VMEM((seqs, slots, width), bf),
            pltpu.VMEM((heads, rows, 128), bf),
            pltpu.VMEM((seqs, slots, 128), bf),
            pltpu.VMEM((seqs, slots, 128), bf),
            pltpu.VMEM((seqs * slots, hidden), f32),
            pltpu.VMEM((seqs * slots, hidden), f32),
            pltpu.VMEM((seqs * slots, hidden), bf),
            dma((seqs,)),
            dma((seqs,)),
            dma((seqs,)),
            dma((seqs,)),
            dma((seqs, subs, 2, nbits)),
            dma((seqs, subs, 2)),
            dma((seqs, subs, 2)),
            dma((seqs, subs, 2)),
            dma((heads,)),
            dma((heads,)),
            dma((heads,)),
            dma((heads,)),
            dma((chunks, heads)),
            dma((chunks, heads)),
            dma((chunks + 1, heads)),
            dma((chunks + 1, heads)),
            dma((chunks + 1, seqs)),
            dma((chunks + 1, seqs)),
            dma((chunks, seqs)),
            dma((chunks, seqs)),
            dma((chunks, heads)),
            dma((chunks, heads)),
            dma((4,)),
            dma((subs, 2)),
            dma((2, chunks, owners)),
            dma((chunks,)),
            dma((chunks + 1,)),
            dma((chunks,)),
        ],
        compiler_params=pltpu.CompilerParams(
            collective_id=0, has_side_effects=True, vmem_limit_bytes=67043328
        ),
    )(
        query,
        key,
        value,
        head_gain.reshape(1, -1),
        out_weight,
        stream,
        model_gain.reshape(1, -1),
        expert_ids,
        expert_gates,
        weight_scales,
        gate_weight,
        up_weight,
        down_weight,
    )


def solution(mesh):
    return jax.shard_map(
        body,
        mesh=mesh,
        in_specs=(
            P("seq", "head"),
            P("seq", "head"),
            P("seq", "head"),
            P("head"),
            P("head", "seq"),
            P(("seq", "head"), None),
            P(),
            P(("seq", "head"), None),
            P(("seq", "head"), None),
            P(("seq", "head"), None, None),
            P(("seq", "head"), None, None),
            P(("seq", "head"), None, None),
            P(("seq", "head"), None),
        ),
        out_specs=P(("seq", "head"), None),
        check_vma=False,
    )
```

```python
import functools

import jax
import jax.numpy as jnp
from jax import lax
from jax.experimental import pallas as pl
from jax.experimental.pallas import tpu as pltpu
from jax.sharding import PartitionSpec as P

HD = 128
SEG = 128
TOPK = 8
MESH = pl.DeviceIdType.MESH


def layer_kernel(
    seqs,
    heads,
    slots,
    q_hbm,
    k_hbm,
    v_hbm,
    gain_ref,
    w_hbm,
    stream_hbm,
    model_ref,
    ids_ref,
    gates_ref,
    scale_ref,
    gate_hbm,
    up_hbm,
    down_hbm,
    out_ref,
    q_ref,
    k_ref,
    v_ref,
    stream_ref,
    state,
    pair_state,
    mixed,
    normed_heads,
    wbuf,
    tot,
    own,
    psend,
    precv,
    res,
    square,
    turn,
    route,
    pick_ref,
    mix_ref,
    gate_v,
    up_v,
    gath,
    send,
    recv,
    back,
    rgath,
    rsend,
    rrecv,
    acc_g,
    acc_u,
    act,
    swap_sem,
    pair_s,
    pair_r,
    fold_sem,
    wls,
    wlr,
    wfs,
    wfr,
    route_sem,
    zs,
    zl,
    zr,
    gs,
    gr,
    ps,
    pr,
    rs,
    rr,
    cs,
    cr,
    load_sem,
    wown_sem,
    wsem,
    dsem,
):
    s = lax.axis_index("seq")
    h = lax.axis_index("head")
    tokens, features = q_ref.shape
    rows, width = stream_ref.shape
    hidden = gate_v.shape[1]
    local = features // HD
    block = w_hbm.shape[1]
    subs = block // SEG
    owners = seqs // 2
    chunks = 2 * subs
    step = owners * SEG
    fine = step // 2
    pieces = 2 * chunks
    halves = 2
    part = features // halves
    bits = [2**i for i in range(1, seqs.bit_length() - 1)]
    orders = [bits, bits[::-1]]
    evens = list(range(0, seqs, 2))
    far = sorted(range(1, seqs), key=lambda d: (-(d // 2).bit_count(), d))
    f32, bf = jnp.float32, jnp.bfloat16
    core = s % 2
    relayed = heads == 4
    inner = (h == 1) | (h == 2)
    low = h // 2
    near = jnp.where(inner, 3 * low, 1 + low)
    other = jnp.where(inner, 3 - h, 2 - low)
    beyond = 3 - near
    first = jnp.where(inner, 1 - low, low)

    def flip(d):
        out, bit = s, 1
        while bit < seqs:
            if d & bit:
                out = out + bit * (1 - 2 * ((s // bit) % 2))
            bit *= 2
        return out

    partner = flip(1)

    def line(d):
        return lax.rem(h + d, heads)

    def cols(c):
        return pl.ds(pl.multiple_of(c * step, step), step)

    def fcols(c):
        return pl.ds(pl.multiple_of(c * fine, fine), fine)

    def seg(c, i):
        return pl.ds(pl.multiple_of(c * step + i * SEG, SEG), SEG)

    def home(c, i):
        at = (2 * i + c % 2) * block + (c // 2) * SEG
        return pl.ds(pl.multiple_of(at, SEG), SEG)

    def settled(ref, sem):
        pltpu.make_async_copy(ref, ref, sem).wait()

    def remote(src, dst, ssem, rsem, seq, head):
        return pltpu.make_async_remote_copy(
            src_ref=src,
            dst_ref=dst,
            send_sem=ssem,
            recv_sem=rsem,
            device_id=(seq, head),
            device_id_type=MESH,
        )

    def share(slot, half):
        return pair_state.at[slot // 2, pl.ds(half * (local // 2), local // 2)]

    def pair_direct(peer):
        at = share(s, core)
        return remote(at, at, pair_s, pair_r.at[s // 2], peer, h)

    def pair_pass(slot):
        at = share(slot, core)
        return remote(at, at, fold_sem.at[0], fold_sem.at[1], partner, h)

    def state_swap():
        return remote(state.at[0], state.at[1], swap_sem.at[0], swap_sem.at[1], partner, h)

    def w_src(j, half):
        return w_hbm.at[pl.ds(half * part, part), pl.ds(pl.multiple_of(j * SEG, SEG), SEG)]

    def w_at(slot, j, half):
        return wbuf.at[
            2 * j + slot % 2,
            pl.ds(half * part, part),
            pl.ds(pl.multiple_of((slot // 2) * SEG, SEG), SEG),
        ]

    def w_send(slot, j, half, bit, source):
        return remote(
            source, w_at(slot, j, half), wls.at[j], wlr.at[slot // 2, j, half], flip(bit), h
        )

    def w_pass(slot, j, half, source):
        return remote(source, w_at(slot, j, half), wfs.at[j], wfr.at[j], partner, h)

    def w_own(j):
        return pltpu.make_async_copy(
            w_hbm.at[:, pl.ds(pl.multiple_of(j * SEG, SEG), SEG)],
            wbuf.at[
                2 * j + core,
                pl.ds(0, features),
                pl.ds(pl.multiple_of((s // 2) * SEG, SEG), SEG),
            ],
            wown_sem.at[j],
        )

    def later_bits(d, half):
        order = orders[half]
        last = max(order.index(bit) for bit in bits if d & bit)
        return order[last + 1 :]

    def w_start(j):
        for i in range(len(bits)):
            for half in range(halves):
                w_send(s, j, half, orders[half][i], w_src(j, half)).start()
        for half in range(halves):
            w_pass(s, j, half, w_src(j, half)).start()

    def w_forward(d, j, half):
        slot = flip(d)
        at = w_at(slot, j, half)
        settled(at, wlr.at[slot // 2, j, half])
        for bit in later_bits(d, half):
            w_send(slot, j, half, bit, at).start()
        w_pass(slot, j, half, at).start()

    def w_near(j):
        for d in evens:
            if d.bit_count() == 1:
                for half in range(halves):
                    w_forward(d, j, half)

    def w_far(j):
        for d in sorted(evens, key=lambda d: (d.bit_count(), d)):
            if d.bit_count() > 1:
                for half in range(halves):
                    w_forward(d, j, half)

    def w_passed(j):
        w_own(j).wait()
        settled(wbuf.at[2 * j + 1 - core, pl.ds(0, features), :], wfr.at[j])

    def w_drain(j):
        settled(
            wbuf.at[2 * j, pl.ds(0, features), pl.ds(0, (owners - 1) * SEG)], wls.at[j]
        )
        settled(wbuf.at[2 * j, pl.ds(0, features), :], wfs.at[j])

    def route_copy(target):
        return remote(route.at[h], route.at[h], route_sem.at[0], route_sem.at[1], s, target)

    def weights(c, i):
        return (
            pltpu.make_async_copy(
                gate_hbm.at[0, home(c, i), :], gate_v.at[seg(c, i), :], wsem.at[0, c]
            ),
            pltpu.make_async_copy(
                up_hbm.at[0, home(c, i), :], up_v.at[seg(c, i), :], wsem.at[1, c]
            ),
        )

    def down_copy(c):
        return pltpu.make_async_copy(
            down_hbm.at[0, :, cols(c)], wbuf.at[c, pl.ds(0, hidden), :], dsem.at[c]
        )

    barrier = pltpu.get_barrier_semaphore()
    for d in range(1, seqs):
        pl.semaphore_signal(barrier, inc=1, device_id=(flip(d), h), device_id_type=MESH)
    for d in range(1, heads):
        pl.semaphore_signal(barrier, inc=1, device_id=(s, line(d)), device_id_type=MESH)
    loads = [
        pltpu.make_async_copy(source, target, load_sem.at[i])
        for i, (source, target) in enumerate(
            [(k_hbm, k_ref), (v_hbm, v_ref), (q_hbm, q_ref), (stream_hbm, stream_ref)]
        )
    ]
    for load in loads:
        load.start()
    pl.semaphore_wait(barrier, seqs + heads - 2)
    w_start(0)
    for n, source in enumerate((ids_ref[...].astype(f32), gates_ref[...])):
        turn[...] = jnp.zeros_like(turn)
        turn[pl.ds(0, TOPK), pl.ds(0, rows)] = source
        route[h, n] = turn[...].T[:rows, :]
    loads[0].wait()
    loads[1].wait()

    def lanes(i):
        return pl.ds(pl.multiple_of(i * HD, HD), HD)

    def block_state(i, carry):
        total = lax.dot_general(
            k_ref[:, lanes(i)], v_ref[:, lanes(i)], (((0,), (0,)), ((), ())),
            preferred_element_type=f32,
        )
        state[0, i] = total.astype(bf)
        return carry

    lax.fori_loop(0, local, block_state, 0)
    state_swap().start()
    for d in range(1, heads):
        route_copy(line(d)).start()

    def own_weights(j, carry):
        w_own(j).start()
        return carry

    lax.fori_loop(0, subs, own_weights, 0)
    state_swap().wait_recv()

    def pair_sum(i, carry):
        pair_state[s // 2, i] = (state[0, i].astype(f32) + state[1, i].astype(f32)).astype(bf)
        return carry

    lax.fori_loop(0, local, pair_sum, 0)
    for d in sorted(evens[1:], key=lambda d: (-d.bit_count(), d)):
        pair_direct(flip(d)).start()

    def start_weights(c, carry):
        for i in range(owners):
            for copy in weights(c, i):
                copy.start()
        return carry

    lax.fori_loop(0, chunks, start_weights, 0)
    loads[2].wait()

    row = lax.broadcasted_iota(jnp.int32, (tokens, tokens), 0)
    col = lax.broadcasted_iota(jnp.int32, (tokens, tokens), 1)
    causal = col <= row

    def local_part(i, carry):
        scores = lax.dot_general(
            q_ref[:, lanes(i)], k_ref[:, lanes(i)], (((1,), (1,)), ((), ())),
            preferred_element_type=f32,
        )
        scores = jnp.where(causal, scores, 0.0).astype(bf)
        mixed[:, lanes(i)] = jnp.dot(scores, v_ref[:, lanes(i)], preferred_element_type=f32)
        return carry

    lax.fori_loop(0, local, local_part, 0)

    w_near(0)
    if subs > 1:
        w_start(1)
    settled(route.at[pl.ds(0, heads - 1)], route_sem.at[1])

    def routing():
        ids = route[:, 0].reshape(tokens, 128)
        gates = route[:, 1].reshape(tokens, 128)
        lane = lax.broadcasted_iota(jnp.int32, (tokens, 128), 1)
        hits = jnp.zeros((tokens, 128), f32)
        shares = jnp.zeros((tokens, 128), f32)
        for n in range(seqs):
            chosen = (ids == (n * heads + h).astype(f32)) & (lane < TOPK)
            hit = jnp.sum(jnp.where(chosen, 1.0, 0.0), axis=1, keepdims=True)
            share = jnp.sum(jnp.where(chosen, gates, 0.0), axis=1, keepdims=True)
            hits = jnp.where(lane == n, hit, hits)
            shares = jnp.where(lane == n, share, shares)
        earlier = jnp.where(col < row, 1.0, 0.0).astype(bf)
        rank = jnp.dot(earlier, hits.astype(bf), preferred_element_type=f32)
        place = jnp.where(hits > 0.5, rank, -1.0)
        spread_row = lax.broadcasted_iota(jnp.int32, (128, seqs * slots), 0)
        spread_col = lax.broadcasted_iota(jnp.int32, (128, seqs * slots), 1)
        inside = (spread_col >= spread_row * slots) & (spread_col < spread_row * slots + slots)
        spread = jnp.where(inside, 1.0, 0.0).astype(bf)
        slot_at = lax.broadcasted_iota(jnp.int32, (tokens, seqs * slots), 1)
        base = jnp.zeros((tokens, seqs * slots), jnp.int32)
        for n in range(1, seqs):
            base = jnp.where(slot_at >= n * slots, n * slots, base)
        slot_at = (slot_at - base).astype(f32)
        taken = jnp.dot(place.astype(bf), spread, preferred_element_type=f32) == slot_at
        shared = jnp.dot(shares.astype(bf), spread, preferred_element_type=f32)
        mix_ref[...] = jnp.where(taken, shared, 0.0).astype(bf)
        pick_ref[...] = jnp.where(taken, 1.0, 0.0).T.astype(bf)

    routing()

    for d in evens[1:]:
        settled(share(flip(d), core), pair_r.at[flip(d) // 2])
        pair_pass(flip(d)).start()
    settled(pair_state.at[pl.ds(0, owners - 1), pl.ds(0, local // 2)], fold_sem.at[1])

    def earlier_part(i, carry):
        prior = jnp.where(core == 1, state[1, i].astype(f32), 0.0)
        for c in range(owners):
            prior = prior + jnp.where(c < s // 2, pair_state[c, i].astype(f32), 0.0)
        total = mixed[:, lanes(i)] + jnp.dot(
            q_ref[:, lanes(i)], prior.astype(bf), preferred_element_type=f32
        )
        mean_square = jnp.mean(total * total, axis=-1, keepdims=True)
        normed_heads[:, lanes(i)] = (
            total * lax.rsqrt(mean_square + 1e-06) * gain_ref[:, lanes(i)]
        ).astype(bf)
        return carry

    lax.fori_loop(0, local, earlier_part, 0)

    def split_heads(total, at, size):
        tot[:, :, pl.ds(0, size)] = total.reshape(heads, rows, size)
        own[:, at] = tot[h, :, pl.ds(0, size)]
        psend[:, :, at] = tot[:, :, pl.ds(0, size)].astype(bf)

    def sum_send(src, dst, sem, target):
        return remote(src, dst, zs, sem, s, target)

    def project(c):
        total = jnp.dot(
            normed_heads[...], wbuf[c, pl.ds(0, features), :], preferred_element_type=f32
        )
        at = cols(c)
        split_heads(total, at, step)
        if not relayed:
            for d in range(1, heads):
                sum_send(
                    psend.at[line(d), :, at], precv.at[h, :, at], zr.at[c], line(d)
                ).start()
            return

        @pl.when(inner)
        def _():
            sum_send(psend.at[near, :, at], precv.at[0, :, at], zr.at[c], near).start()

        @pl.when(jnp.logical_not(inner))
        def _():
            sum_send(
                psend.at[pl.ds(1 - low, 3), :, at], precv.at[pl.ds(0, 3), :, at], zl.at[c], near
            ).start()

    def merge(c):
        if not relayed:
            return
        at = cols(c)

        @pl.when(inner)
        def _():
            settled(precv.at[pl.ds(0, 3), :, at], zl.at[c])
            for target, slot in ((other, 3), (beyond, 1)):
                merged = psend[target, :, at].astype(f32) + precv[
                    target - first, :, at
                ].astype(f32)
                psend[target, :, at] = merged.astype(bf)
                sum_send(
                    psend.at[target, :, at], precv.at[slot, :, at], zr.at[c], target
                ).start()

    def gather_send(src, c, target):
        return remote(src, src, gs.at[0], gr.at[c], s, target)

    def settle(c):
        if relayed:

            @pl.when(inner)
            def _():
                settled(precv.at[3, :, cols(c)], zr.at[c])

            @pl.when(jnp.logical_not(inner))
            def _():
                settled(precv.at[pl.ds(0, 2), :, cols(c)], zr.at[c])

            sources = [jnp.where(inner, h - first, 0), jnp.where(inner, 3, 1)]
        else:
            settled(precv.at[pl.ds(0, heads - 1), :, cols(c)], zr.at[c])
            sources = [line(d) for d in range(1, heads)]
        for i in range(owners):
            total = own[:, seg(c, i)]
            for source in sources:
                total = total + precv[source, :, seg(c, i)].astype(f32)
            residual = (stream_ref[:, home(c, i)].astype(f32) + total).astype(bf)
            res[:, home(c, i)] = residual
            value = residual.astype(f32)
            square[...] += value * value
            gath[h, :, seg(c, i)] = (value * model_ref[:, home(c, i)]).astype(bf)
        for target in (near, other) if relayed else [line(d) for d in range(1, heads)]:
            gather_send(gath.at[h, :, cols(c)], c, target).start()

    def pass_on(c):
        if not relayed:
            return

        @pl.when(inner)
        def _():
            settled(gath.at[pl.ds(0, 3), :, cols(c)], gr.at[c])
            gather_send(gath.at[pl.ds(2 - 2 * low, 2), :, cols(c)], c, near).start()

    def settle_norm():
        mean_square = jnp.sum(square[...], axis=1, keepdims=True) / width
        factor = jnp.broadcast_to(lax.rsqrt(mean_square + 1e-06), (rows, 128))
        high = factor.astype(bf).astype(f32)
        rest = (factor - high).astype(bf).astype(f32)
        at = lax.broadcasted_iota(jnp.int32, (rows, 128), 1)
        rgath[h] = jnp.where(at < 64, high, rest).astype(bf)
        for d in range(1, heads):
            at = rgath.at[h]
            remote(at, at, gs.at[1], gr.at[chunks], s, line(d)).start()

    def own_copy(c):
        return pltpu.make_async_copy(send.at[s, :, cols(c)], recv.at[s, :, cols(c)], pr.at[c])

    def dispatch(c):
        def arrived():
            settled(gath.at[pl.ds(0, heads - 1), :, cols(c)], gr.at[c])

        if relayed:
            pl.when(jnp.logical_not(inner))(arrived)
        else:
            arrived()
        picked = jnp.dot(
            pick_ref[...], gath[:, :, cols(c)].reshape(tokens, step),
            preferred_element_type=f32,
        )
        send[:, :, cols(c)] = picked.astype(bf).reshape(seqs, slots, step)
        for d in far:
            remote(
                send.at[flip(d), :, cols(c)], recv.at[s, :, cols(c)], ps.at[0], pr.at[c],
                flip(d), h,
            ).start()
        own_copy(c).start()

    def dispatch_norm():
        settled(rgath.at[pl.ds(0, heads - 1)], gr.at[chunks])
        picked = jnp.dot(
            pick_ref[...], rgath[...].reshape(tokens, 128), preferred_element_type=f32
        )
        rsend[...] = picked.astype(bf).reshape(seqs, slots, 128)
        for d in far:
            remote(
                rsend.at[flip(d)], rrecv.at[s], ps.at[1], pr.at[chunks], flip(d), h
            ).start()
        pltpu.make_async_copy(rsend.at[s], rrecv.at[s], pr.at[chunks]).start()

    def expand(c):
        pltpu.make_async_copy(
            gate_hbm.at[0, pl.ds(0, step), :], gate_v.at[cols(c), :], wsem.at[0, c]
        ).wait()
        pltpu.make_async_copy(
            up_hbm.at[0, pl.ds(0, step), :], up_v.at[cols(c), :], wsem.at[1, c]
        ).wait()
        settled(recv.at[:, :, cols(c)], pr.at[c])
        lhs = recv[:, :, cols(c)].reshape(seqs * slots, step)
        acc_g[...] += jnp.dot(lhs, gate_v[cols(c), :], preferred_element_type=f32)
        acc_u[...] += jnp.dot(lhs, up_v[cols(c), :], preferred_element_type=f32)

    acc_g[...] = jnp.zeros_like(acc_g)
    acc_u[...] = jnp.zeros_like(acc_u)
    square[...] = jnp.zeros_like(square)
    loads[3].wait()

    w_far(0)
    w_passed(0)
    depth = 6

    def stage(t, lag, work):
        @pl.when((t >= lag) & (t < chunks + lag))
        def _():
            work(t - lag)

    def forward(t, carry):
        j = (t + 2) // 2

        @pl.when((t % 2 == 0) & (j < subs))
        def _():
            w_near(j)

        @pl.when((t % 2 == 0) & (j + 1 < subs))
        def _():
            w_start(j + 1)

        @pl.when((t % 2 == 1) & (j < subs))
        def _():
            w_far(j)
            w_passed(j)

        stage(t, 4, dispatch)
        stage(t, 3, pass_on)
        stage(t, 2, settle)

        @pl.when(t == chunks + 1)
        def _():
            settle_norm()

        stage(t, 1, merge)
        stage(t, 0, project)

        @pl.when(t == chunks + 3)
        def _():
            dispatch_norm()

        stage(t, depth, expand)
        return carry

    lax.fori_loop(0, chunks + depth, forward, 0)

    def release(j, carry):
        w_drain(j)
        return carry

    def start_down(c, carry):
        down_copy(c).start()
        return carry

    lax.fori_loop(0, subs, release, 0)
    lax.fori_loop(0, chunks, start_down, 0)
    settled(psend.at[pl.ds(0, heads - 1)], zs)
    settled(rrecv, pr.at[chunks])
    gate_scale = scale_ref[0, 0]
    up_scale = scale_ref[0, 1]
    down_scale = scale_ref[0, 2]

    def activate(i, carry):
        at = pl.ds(pl.multiple_of(i * slots, slots), slots)
        factor = jnp.sum(rrecv[i].astype(f32), axis=1, keepdims=True) / 64
        g = acc_g[at, :] * (factor * gate_scale)
        u = acc_u[at, :] * (factor * up_scale)
        act[at, :] = (g / (1.0 + jnp.exp(-g)) * u).astype(bf)
        return carry

    lax.fori_loop(0, seqs, activate, 0)

    def contract(c, carry):
        @pl.when(c % 2 == 0)
        def _():
            down_copy(c // 2).wait()

        at = fcols(c)
        rows_out = jnp.dot(
            act[...],
            wbuf[c // 2, pl.ds(0, hidden), pl.ds(pl.multiple_of((c % 2) * fine, fine), fine)],
            preferred_element_type=f32,
        )
        recv[:, :, at] = (rows_out * down_scale).astype(bf).reshape(seqs, slots, fine)
        for d in far:
            remote(
                recv.at[flip(d), :, at], back.at[s, :, at], rs, rr.at[c], flip(d), h
            ).start()
        pltpu.make_async_copy(recv.at[s, :, at], back.at[s, :, at], rr.at[c]).start()
        return carry

    lax.fori_loop(0, pieces, contract, 0)

    def combine(c):
        at = fcols(c)
        settled(back.at[:, :, at], rr.at[c])
        total = jnp.dot(
            mix_ref[...], back[:, :, at].reshape(seqs * slots, fine),
            preferred_element_type=f32,
        )
        split_heads(total, at, fine)
        for d in range(1, heads):
            remote(
                psend.at[line(d), :, at], precv.at[h, :, at], cs, cr.at[c], s, line(d)
            ).start()

    def finish(c):
        at = fcols(c)
        settled(precv.at[pl.ds(0, heads - 1), :, at], cr.at[c])
        total = res[:, at].astype(f32) + own[:, at]
        for d in range(1, heads):
            total = total + precv[line(d), :, at].astype(f32)
        out_ref[:, at] = total.astype(bf)

    def backward(t, carry):
        @pl.when(t < pieces)
        def _():
            combine(t)

        @pl.when(t >= 2)
        def _():
            finish(t - 2)

        return carry

    lax.fori_loop(0, pieces + 2, backward, 0)

    state_swap().wait_send()
    settled(pair_state.at[pl.ds(0, owners - 1), pl.ds(0, local // 2)], pair_s)
    settled(pair_state.at[pl.ds(0, owners - 1), pl.ds(0, local // 2)], fold_sem.at[0])
    settled(route.at[pl.ds(0, heads - 1)], route_sem.at[0])
    if relayed:

        @pl.when(inner)
        def _():
            settled(gath, gs.at[0])

        @pl.when(jnp.logical_not(inner))
        def _():
            settled(gath.at[pl.ds(0, 2)], gs.at[0])
    else:
        settled(gath.at[pl.ds(0, heads - 1)], gs.at[0])
    settled(rgath.at[pl.ds(0, heads - 1)], gs.at[1])
    settled(send.at[pl.ds(0, seqs - 1)], ps.at[0])
    settled(rsend.at[pl.ds(0, seqs - 1)], ps.at[1])
    settled(recv.at[pl.ds(0, seqs - 1)], rs)
    settled(psend.at[pl.ds(0, heads - 1)], cs)


def body(
    query,
    key,
    value,
    head_gain,
    out_weight,
    stream,
    model_gain,
    expert_ids,
    expert_gates,
    gate_weight,
    up_weight,
    down_weight,
    weight_scales,
):
    seqs, heads = lax.axis_size("seq"), lax.axis_size("head")
    tokens, features = query.shape
    rows, width = stream.shape
    hidden = gate_weight.shape[2]
    local = features // HD
    block = out_weight.shape[1]
    subs = block // SEG
    owners = seqs // 2
    chunks = 2 * subs
    step = owners * SEG
    capacity = 3 * rows * TOPK // (2 * seqs * heads)
    slots = -(-capacity * heads // 16) * 16
    vmem = pl.BlockSpec(memory_space=pltpu.VMEM)
    smem = pl.BlockSpec(memory_space=pltpu.SMEM)
    anywhere = pl.BlockSpec(memory_space=pl.ANY)
    bf, f32 = jnp.bfloat16, jnp.float32
    dma = pltpu.SemaphoreType.DMA
    return pl.pallas_call(
        functools.partial(layer_kernel, seqs, heads, slots),
        out_shape=jax.ShapeDtypeStruct((rows, width), bf),
        in_specs=[anywhere] * 3 + [vmem] + [anywhere] * 2 + [vmem] * 3 + [smem] + [anywhere] * 3,
        out_specs=vmem,
        scratch_shapes=[
            pltpu.VMEM((tokens, features), bf),
            pltpu.VMEM((tokens, features), bf),
            pltpu.VMEM((tokens, features), bf),
            pltpu.VMEM((rows, width), bf),
            pltpu.VMEM((2, local, HD, HD), bf),
            pltpu.VMEM((owners, local, HD, HD), bf),
            pltpu.VMEM((tokens, features), f32),
            pltpu.VMEM((tokens, features), bf),
            pltpu.VMEM((chunks, max(features, hidden), step), bf),
            pltpu.VMEM((heads, rows, step), f32),
            pltpu.VMEM((rows, width), f32),
            pltpu.VMEM((heads, rows, width), bf),
            pltpu.VMEM((heads, rows, width), bf),
            pltpu.VMEM((rows, width), bf),
            pltpu.VMEM((rows, SEG), f32),
            pltpu.VMEM((128, 128), f32),
            pltpu.VMEM((heads, 2, rows, 128), f32),
            pltpu.VMEM((seqs * slots, tokens), bf),
            pltpu.VMEM((tokens, seqs * slots), bf),
            pltpu.VMEM((width, hidden), bf),
            pltpu.VMEM((width, hidden), bf),
            pltpu.VMEM((heads, rows, width), bf),
            pltpu.VMEM((seqs, slots, width), bf),
            pltpu.VMEM((seqs, slots, width), bf),
            pltpu.VMEM((seqs, slots, width), bf),
            pltpu.VMEM((heads, rows, 128), bf),
            pltpu.VMEM((seqs, slots, 128), bf),
            pltpu.VMEM((seqs, slots, 128), bf),
            pltpu.VMEM((seqs * slots, hidden), f32),
            pltpu.VMEM((seqs * slots, hidden), f32),
            pltpu.VMEM((seqs * slots, hidden), bf),
            dma((2,)),
            dma,
            dma((owners,)),
            dma((2,)),
            dma((subs,)),
            dma((owners, subs, 2)),
            dma((subs,)),
            dma((subs,)),
            dma((2,)),
            dma,
            dma((chunks,)),
            dma((chunks,)),
            dma((2,)),
            dma((chunks + 1,)),
            dma((2,)),
            dma((chunks + 1,)),
            dma,
            dma((2 * chunks,)),
            dma,
            dma((2 * chunks,)),
            dma((4,)),
            dma((subs,)),
            dma((2, chunks)),
            dma((chunks,)),
        ],
        compiler_params=pltpu.CompilerParams(
            collective_id=0, has_side_effects=True, vmem_limit_bytes=67043328
        ),
    )(
        query,
        key,
        value,
        head_gain.reshape(1, -1),
        out_weight,
        stream,
        model_gain.reshape(1, -1),
        expert_ids.T,
        expert_gates.T,
        weight_scales,
        gate_weight,
        up_weight,
        down_weight,
    )


def solution(mesh):
    return jax.shard_map(
        body,
        mesh=mesh,
        in_specs=(
            P("seq", "head"),
            P("seq", "head"),
            P("seq", "head"),
            P("head"),
            P("head", "seq"),
            P(("seq", "head"), None),
            P(),
            P(("seq", "head"), None),
            P(("seq", "head"), None),
            P(("seq", "head"), None, None),
            P(("seq", "head"), None, None),
            P(("seq", "head"), None, None),
            P(("seq", "head"), None),
        ),
        out_specs=P(("seq", "head"), None),
        check_vma=False,
    )
```

```python
import functools

import jax
import jax.numpy as jnp
from jax import lax
from jax.experimental import pallas as pl
from jax.experimental.pallas import tpu as pltpu
from jax.sharding import PartitionSpec as P

HD = 128
SEG = 128
TOPK = 8
MESH = pl.DeviceIdType.MESH


def layer_kernel(
    seqs,
    heads,
    slots,
    q_hbm,
    k_hbm,
    v_hbm,
    gain_ref,
    w_hbm,
    stream_hbm,
    model_ref,
    ids_ref,
    gates_ref,
    scale_ref,
    gate_hbm,
    up_hbm,
    down_hbm,
    out_ref,
    q_ref,
    k_ref,
    v_ref,
    stream_ref,
    state,
    pair_state,
    normed_heads,
    wbuf,
    tot,
    own,
    psend,
    precv,
    res,
    square,
    turn,
    route,
    near_route,
    table,
    pick_ref,
    mix_ref,
    gate_v,
    up_v,
    gath,
    nbr,
    send,
    recv,
    back,
    rgath,
    rnbr,
    rsend,
    rrecv,
    acc_g,
    acc_u,
    act,
    swap_sem,
    pair_s,
    pair_r,
    fold_sem,
    wls,
    wlr,
    wfs,
    wfr,
    route_sem,
    near_s,
    near_r,
    zs,
    zl,
    zr,
    gs,
    gr,
    ds,
    nr,
    ps,
    pr,
    rs,
    rr,
    rl,
    es,
    er,
    cs,
    cr,
    load_sem,
    wown_sem,
    wsem,
    dsem,
):
    s = lax.axis_index("seq")
    h = lax.axis_index("head")
    tokens, features = q_ref.shape
    rows, width = stream_ref.shape
    hidden = gate_v.shape[1]
    local = features // HD
    block = w_hbm.shape[1]
    subs = block // SEG
    owners = seqs // 2
    chunks = 2 * subs
    step = owners * SEG
    fine = step // 2
    pieces = 2 * chunks
    halves = 2
    part = features // halves
    bits = [2**i for i in range(1, seqs.bit_length() - 1)]
    orders = [bits, bits[::-1]]
    evens = list(range(0, seqs, 2))
    woven = seqs == 8
    ways = [(2, 4), (4, 2)] if woven else [(0, 0)]
    lists = [[0, 1, b2, b2 + 1] for _, b2 in ways] if woven else [list(range(seqs))]
    count = len(lists[0])
    owned = count * slots
    f32, bf = jnp.float32, jnp.bfloat16
    core = s % 2
    relayed = heads == 4
    inner = (h == 1) | (h == 2)
    low = h // 2
    near = jnp.where(inner, 3 * low, 1 + low)
    other = jnp.where(inner, 3 - h, 2 - low)
    beyond = 3 - near
    first = jnp.where(inner, 1 - low, low)

    def flip(d):
        out, bit = s, 1
        while bit < seqs:
            if d & bit:
                out = out + bit * (1 - 2 * ((s // bit) % 2))
            bit *= 2
        return out

    partner = flip(1)

    def line(d):
        return lax.rem(h + d, heads)

    def cols(c):
        return pl.ds(pl.multiple_of(c * step, step), step)

    def fcols(c):
        return pl.ds(pl.multiple_of(c * fine, fine), fine)

    def seg(c, i):
        return pl.ds(pl.multiple_of(c * step + i * SEG, SEG), SEG)

    def home(c, i):
        at = (2 * i + c % 2) * block + (c // 2) * SEG
        return pl.ds(pl.multiple_of(at, SEG), SEG)

    def band(i, n=1):
        return pl.ds(pl.multiple_of(i * rows, rows), n * rows)

    def settled(ref, sem):
        pltpu.make_async_copy(ref, ref, sem).wait()

    def remote(src, dst, ssem, rsem, seq, head):
        return pltpu.make_async_remote_copy(
            src_ref=src,
            dst_ref=dst,
            send_sem=ssem,
            recv_sem=rsem,
            device_id=(seq, head),
            device_id_type=MESH,
        )

    def share(slot, half):
        return pair_state.at[slot // 2, pl.ds(half * (local // 2), local // 2)]

    def pair_direct(peer):
        at = share(s, core)
        return remote(at, at, pair_s, pair_r.at[s // 2], peer, h)

    def pair_pass(slot):
        at = share(slot, core)
        return remote(at, at, fold_sem.at[0], fold_sem.at[1], partner, h)

    def state_swap():
        return remote(state.at[0], state.at[1], swap_sem.at[0], swap_sem.at[1], partner, h)

    def w_src(j, half):
        return w_hbm.at[pl.ds(half * part, part), pl.ds(pl.multiple_of(j * SEG, SEG), SEG)]

    def w_at(slot, j, half):
        return wbuf.at[
            2 * j + slot % 2,
            pl.ds(half * part, part),
            pl.ds(pl.multiple_of((slot // 2) * SEG, SEG), SEG),
        ]

    def w_send(slot, j, half, bit, source):
        return remote(
            source, w_at(slot, j, half), wls.at[j], wlr.at[slot // 2, j, half], flip(bit), h
        )

    def w_pass(slot, j, half, source):
        return remote(source, w_at(slot, j, half), wfs.at[j], wfr.at[j], partner, h)

    def w_own(j):
        return pltpu.make_async_copy(
            w_hbm.at[:, pl.ds(pl.multiple_of(j * SEG, SEG), SEG)],
            wbuf.at[
                2 * j + core,
                pl.ds(0, features),
                pl.ds(pl.multiple_of((s // 2) * SEG, SEG), SEG),
            ],
            wown_sem.at[j],
        )

    def later_bits(d, half):
        order = orders[half]
        last = max(order.index(bit) for bit in bits if d & bit)
        return order[last + 1 :]

    def w_start(j):
        for i in range(len(bits)):
            for half in range(halves):
                w_send(s, j, half, orders[half][i], w_src(j, half)).start()
        for half in range(halves):
            w_pass(s, j, half, w_src(j, half)).start()

    def w_forward(d, j, half):
        slot = flip(d)
        at = w_at(slot, j, half)
        settled(at, wlr.at[slot // 2, j, half])
        for bit in later_bits(d, half):
            w_send(slot, j, half, bit, at).start()
        w_pass(slot, j, half, at).start()

    def w_near(j):
        for d in evens:
            if d.bit_count() == 1:
                for half in range(halves):
                    w_forward(d, j, half)

    def w_far(j):
        for d in sorted(evens, key=lambda d: (d.bit_count(), d)):
            if d.bit_count() > 1:
                for half in range(halves):
                    w_forward(d, j, half)

    def w_passed(j):
        w_own(j).wait()
        settled(wbuf.at[2 * j + 1 - core, pl.ds(0, features), :], wfr.at[j])

    def w_drain(j):
        settled(
            wbuf.at[2 * j, pl.ds(0, features), pl.ds(0, (owners - 1) * SEG)], wls.at[j]
        )
        settled(wbuf.at[2 * j, pl.ds(0, features), :], wfs.at[j])

    def route_copy(target):
        return remote(route.at[h], route.at[h], route_sem.at[0], route_sem.at[1], s, target)

    def weights(c, i):
        return (
            pltpu.make_async_copy(
                gate_hbm.at[0, home(c, i), :], gate_v.at[seg(c, i), :], wsem.at[0, c]
            ),
            pltpu.make_async_copy(
                up_hbm.at[0, home(c, i), :], up_v.at[seg(c, i), :], wsem.at[1, c]
            ),
        )

    def down_copy(c):
        return pltpu.make_async_copy(
            down_hbm.at[0, :, cols(c)], wbuf.at[c, pl.ds(0, hidden), :], dsem.at[c]
        )

    barrier = pltpu.get_barrier_semaphore()
    for d in range(1, seqs):
        pl.semaphore_signal(barrier, inc=1, device_id=(flip(d), h), device_id_type=MESH)
    for d in range(1, heads):
        pl.semaphore_signal(barrier, inc=1, device_id=(s, line(d)), device_id_type=MESH)
    loads = [
        pltpu.make_async_copy(source, target, load_sem.at[i])
        for i, (source, target) in enumerate(
            [(k_hbm, k_ref), (v_hbm, v_ref), (q_hbm, q_ref), (stream_hbm, stream_ref)]
        )
    ]
    for load in loads:
        load.start()
    pl.semaphore_wait(barrier, seqs + heads - 2)
    w_start(0)
    route[h] = jnp.zeros((2 * TOPK, 128), f32)
    route[h, pl.ds(0, TOPK), pl.ds(0, rows)] = ids_ref[...].astype(f32)
    route[h, pl.ds(TOPK, TOPK), pl.ds(0, rows)] = gates_ref[...]
    loads[0].wait()
    loads[1].wait()

    def lanes(i):
        return pl.ds(pl.multiple_of(i * HD, HD), HD)

    def mixed(i):
        across = hidden // HD
        return (
            pl.ds(pl.multiple_of((i // across) * tokens, tokens), tokens),
            pl.ds(pl.multiple_of((i % across) * HD, HD), HD),
        )

    def block_state(i, carry):
        total = lax.dot_general(
            k_ref[:, lanes(i)], v_ref[:, lanes(i)], (((0,), (0,)), ((), ())),
            preferred_element_type=f32,
        )
        state[0, i] = total.astype(bf)
        return carry

    lax.fori_loop(0, local, block_state, 0)
    state_swap().start()
    for d in range(1, heads):
        route_copy(line(d)).start()

    def own_weights(j, carry):
        w_own(j).start()
        return carry

    lax.fori_loop(0, subs, own_weights, 0)
    state_swap().wait_recv()

    def pair_sum(i, carry):
        pair_state[s // 2, i] = (state[0, i].astype(f32) + state[1, i].astype(f32)).astype(bf)
        return carry

    lax.fori_loop(0, local, pair_sum, 0)
    for d in sorted(evens[1:], key=lambda d: (-d.bit_count(), d)):
        pair_direct(flip(d)).start()

    def start_weights(c, carry):
        for i in range(owners):
            for copy in weights(c, i):
                copy.start()
        return carry

    lax.fori_loop(0, chunks, start_weights, 0)
    loads[2].wait()

    row = lax.broadcasted_iota(jnp.int32, (tokens, tokens), 0)
    col = lax.broadcasted_iota(jnp.int32, (tokens, tokens), 1)
    causal = col <= row

    def local_part(i, carry):
        scores = lax.dot_general(
            q_ref[:, lanes(i)], k_ref[:, lanes(i)], (((1,), (1,)), ((), ())),
            preferred_element_type=f32,
        )
        scores = jnp.where(causal, scores, 0.0).astype(bf)
        acc_g[mixed(i)] = jnp.dot(scores, v_ref[:, lanes(i)], preferred_element_type=f32)
        return carry

    lax.fori_loop(0, local, local_part, 0)

    w_near(0)
    if subs > 1:
        w_start(1)
    settled(route.at[pl.ds(0, heads - 1)], route_sem.at[1])
    if woven:
        for o, (b1, _) in enumerate(ways):
            remote(route, near_route.at[o], near_s, near_r.at[o], flip(b1), h).start()

    def tables(o, who):
        def turned(i, carry):
            turn[...] = jnp.zeros_like(turn)
            source = near_route.at[o, i] if who else route.at[i]
            turn[pl.ds(0, TOPK), :] = source[pl.ds(0, TOPK), :]
            turn[pl.ds(64, TOPK), :] = source[pl.ds(TOPK, TOPK), :]
            table[i] = turn[...].T[:rows, :]
            return carry

        lax.fori_loop(0, heads, turned, 0)
        ids = table[...].reshape(tokens, 128)
        gates = pltpu.roll(ids, 64, 1)
        lane = lax.broadcasted_iota(jnp.int32, (tokens, 128), 1)
        hits = jnp.zeros((tokens, 128), f32)
        shares = jnp.zeros((tokens, 128), f32)
        for n, d in enumerate(lists[o]):
            expert = flip(d) * heads + h
            chosen = (ids == expert.astype(f32)) & (lane < TOPK)
            hit = jnp.sum(jnp.where(chosen, 1.0, 0.0), axis=1, keepdims=True)
            share = jnp.sum(jnp.where(chosen, gates, 0.0), axis=1, keepdims=True)
            hits = jnp.where(lane == n, hit, hits)
            shares = jnp.where(lane == n, share, shares)
        earlier = jnp.where(col < row, 1.0, 0.0).astype(bf)
        rank = jnp.dot(earlier, hits.astype(bf), preferred_element_type=f32)
        place = jnp.where(hits > 0.5, rank, -1.0)
        spread_row = lax.broadcasted_iota(jnp.int32, (128, owned), 0)
        spread_col = lax.broadcasted_iota(jnp.int32, (128, owned), 1)
        inside = (spread_col >= spread_row * slots) & (spread_col < spread_row * slots + slots)
        spread = jnp.where(inside, 1.0, 0.0).astype(bf)
        slot_at = lax.broadcasted_iota(jnp.int32, (tokens, owned), 1)
        base = jnp.zeros((tokens, owned), jnp.int32)
        for n in range(1, count):
            base = jnp.where(slot_at >= n * slots, n * slots, base)
        slot_at = (slot_at - base).astype(f32)
        taken = jnp.dot(place.astype(bf), spread, preferred_element_type=f32) == slot_at
        shared = jnp.dot(shares.astype(bf), spread, preferred_element_type=f32)
        mix_ref[o, who] = jnp.where(taken, shared, 0.0).astype(bf)
        pick_ref[o, who] = jnp.where(taken, 1.0, 0.0).T.astype(bf)

    def routing():
        if woven:
            for o in range(2):
                settled(near_route.at[o], near_r.at[o])
        for o in range(len(ways)):
            for who in range(2 if woven else 1):
                tables(o, who)

    for d in evens[1:]:
        settled(share(flip(d), core), pair_r.at[flip(d) // 2])
        pair_pass(flip(d)).start()
    settled(pair_state.at[pl.ds(0, owners - 1), pl.ds(0, local // 2)], fold_sem.at[1])

    def earlier_part(i, carry):
        prior = jnp.where(core == 1, state[1, i].astype(f32), 0.0)
        for c in range(owners):
            prior = prior + jnp.where(c < s // 2, pair_state[c, i].astype(f32), 0.0)
        total = acc_g[mixed(i)] + jnp.dot(
            q_ref[:, lanes(i)], prior.astype(bf), preferred_element_type=f32
        )
        mean_square = jnp.mean(total * total, axis=-1, keepdims=True)
        normed_heads[:, lanes(i)] = (
            total * lax.rsqrt(mean_square + 1e-06) * gain_ref[:, lanes(i)]
        ).astype(bf)
        return carry

    lax.fori_loop(0, local, earlier_part, 0)

    def split_heads(total, at, size):
        tot[:, :, pl.ds(0, size)] = total.reshape(heads, rows, size)
        own[:, at] = tot[h, :, pl.ds(0, size)]
        psend[:, :, at] = tot[:, :, pl.ds(0, size)].astype(bf)

    def sum_send(src, dst, sem, target):
        return remote(src, dst, zs, sem, s, target)

    def project(c):
        total = jnp.dot(
            normed_heads[...], wbuf[c, pl.ds(0, features), :], preferred_element_type=f32
        )
        at = cols(c)
        split_heads(total, at, step)
        if not relayed:
            for d in range(1, heads):
                sum_send(
                    psend.at[line(d), :, at], precv.at[h, :, at], zr.at[c], line(d)
                ).start()
            return

        @pl.when(inner)
        def _():
            sum_send(psend.at[near, :, at], precv.at[0, :, at], zr.at[c], near).start()

        @pl.when(jnp.logical_not(inner))
        def _():
            sum_send(
                psend.at[pl.ds(1 - low, 3), :, at], precv.at[pl.ds(0, 3), :, at], zl.at[c], near
            ).start()

    def merge(c):
        if not relayed:
            return
        at = cols(c)

        @pl.when(inner)
        def _():
            settled(precv.at[pl.ds(0, 3), :, at], zl.at[c])
            for target, slot in ((other, 3), (beyond, 1)):
                merged = psend[target, :, at].astype(f32) + precv[
                    target - first, :, at
                ].astype(f32)
                psend[target, :, at] = merged.astype(bf)
                sum_send(
                    psend.at[target, :, at], precv.at[slot, :, at], zr.at[c], target
                ).start()

    def gather_send(src, c, target):
        return remote(src, src, gs.at[0], gr.at[c], s, target)

    def settle(c):
        if relayed:

            @pl.when(inner)
            def _():
                settled(precv.at[3, :, cols(c)], zr.at[c])

            @pl.when(jnp.logical_not(inner))
            def _():
                settled(precv.at[pl.ds(0, 2), :, cols(c)], zr.at[c])

            sources = [jnp.where(inner, h - first, 0), jnp.where(inner, 3, 1)]
        else:
            settled(precv.at[pl.ds(0, heads - 1), :, cols(c)], zr.at[c])
            sources = [line(d) for d in range(1, heads)]
        for i in range(owners):
            total = own[:, seg(c, i)]
            for source in sources:
                total = total + precv[source, :, seg(c, i)].astype(f32)
            residual = (stream_ref[:, home(c, i)].astype(f32) + total).astype(bf)
            res[:, home(c, i)] = residual
            value = residual.astype(f32)
            square[...] += value * value
            gath[band(h), seg(c, i)] = (value * model_ref[:, home(c, i)]).astype(bf)
        for target in (near, other) if relayed else [line(d) for d in range(1, heads)]:
            gather_send(gath.at[band(h), cols(c)], c, target).start()

    def pass_on(c):
        if not relayed:
            return

        @pl.when(inner)
        def _():
            settled(gath.at[band(0, 3), cols(c)], gr.at[c])
            gather_send(gath.at[band(2 - 2 * low, 2), cols(c)], c, near).start()

    def settle_norm():
        mean_square = jnp.sum(square[...], axis=1, keepdims=True) / width
        factor = jnp.broadcast_to(lax.rsqrt(mean_square + 1e-06), (rows, 128))
        high = factor.astype(bf).astype(f32)
        rest = (factor - high).astype(bf).astype(f32)
        at = lax.broadcasted_iota(jnp.int32, (rows, 128), 1)
        rgath[band(h), :] = jnp.where(at < 64, high, rest).astype(bf)
        for d in range(1, heads):
            at = rgath.at[band(h), :]
            remote(at, at, gs.at[1], gr.at[chunks], s, line(d)).start()

    def choose(c, work):
        if not woven:
            work(0)
            return
        for o in range(2):

            @pl.when(c % 2 == o)
            def _(o=o):
                work(o)

    def scatter(o, who, source, size, at, c, buffers):
        out, target, psem, _ = buffers
        picked = jnp.dot(pick_ref[o, who], source, preferred_element_type=f32)
        here = pl.ds(who * count, count)
        out[here, :, at] = picked.astype(bf).reshape(count, slots, size)
        b1 = ways[o][0] if who else 0
        order = range(count - 1, -1, -1)
        for n in order:
            d = lists[o][n]
            src = out.at[who * count + n, :, at]
            dst = target.at[d ^ b1, :, at]
            if d == 0:
                pltpu.make_async_copy(src, dst, pr.at[c]).start()
            else:
                remote(src, dst, psem, pr.at[c], flip(d), h).start()

    def spread_rows(o, gathered, beside, at, size, c, buffers):
        dsem = buffers[3]
        if woven:
            remote(
                gathered.at[:, at], beside.at[:, at], dsem, nr.at[c], flip(ways[o][0]), h
            ).start()
        scatter(o, 0, gathered[:, at], size, at, c, buffers)

    def relay_rows(o, beside, at, size, c, buffers):
        settled(beside.at[:, at], nr.at[c])
        scatter(o, 1, beside[:, at], size, at, c, buffers)

    def dispatch(c):
        def arrived():
            settled(gath.at[band(0, heads - 1), cols(c)], gr.at[c])

        if relayed:
            pl.when(jnp.logical_not(inner))(arrived)
        else:
            arrived()
        choose(c, lambda o: spread_rows(o, gath, nbr, cols(c), step, c, (send, recv, ps.at[0], ds.at[0])))

    def relay(c):
        if woven:
            choose(c, lambda o: relay_rows(o, nbr, cols(c), step, c, (send, recv, ps.at[0], ds.at[0])))

    def dispatch_norm():
        settled(rgath.at[band(0, heads - 1), :], gr.at[chunks])
        spread_rows(0, rgath, rnbr, pl.ds(0, 128), 128, chunks, (rsend, rrecv, ps.at[1], ds.at[1]))

    def relay_norm():
        if woven:
            relay_rows(0, rnbr, pl.ds(0, 128), 128, chunks, (rsend, rrecv, ps.at[1], ds.at[1]))

    def expand(c):
        pltpu.make_async_copy(
            gate_hbm.at[0, pl.ds(0, step), :], gate_v.at[cols(c), :], wsem.at[0, c]
        ).wait()
        pltpu.make_async_copy(
            up_hbm.at[0, pl.ds(0, step), :], up_v.at[cols(c), :], wsem.at[1, c]
        ).wait()
        settled(recv.at[:, :, cols(c)], pr.at[c])
        lhs = recv[:, :, cols(c)].reshape(seqs * slots, step)
        acc_g[...] += jnp.dot(lhs, gate_v[cols(c), :], preferred_element_type=f32)
        acc_u[...] += jnp.dot(lhs, up_v[cols(c), :], preferred_element_type=f32)

    acc_g[...] = jnp.zeros_like(acc_g)
    acc_u[...] = jnp.zeros_like(acc_u)
    square[...] = jnp.zeros_like(square)
    loads[3].wait()

    w_far(0)
    w_passed(0)
    depth = 7 if woven else 6

    def stage(t, lag, work):
        @pl.when((t >= lag) & (t < chunks + lag))
        def _():
            work(t - lag)

    def release(j, carry):
        w_drain(j)
        return carry

    def forward(t, carry):
        j = (t + 2) // 2

        @pl.when((t % 2 == 0) & (j < subs))
        def _():
            w_near(j)

        @pl.when((t % 2 == 0) & (j + 1 < subs))
        def _():
            w_start(j + 1)

        @pl.when((t % 2 == 1) & (j < subs))
        def _():
            w_far(j)
            w_passed(j)

        stage(t, 4, dispatch)
        stage(t, 5, relay)
        stage(t, 3, pass_on)
        stage(t, 2, settle)

        @pl.when(t == chunks + 1)
        def _():
            settle_norm()

        stage(t, 1, merge)
        stage(t, 0, project)

        @pl.when(t == 0)
        def _():
            routing()

        @pl.when(t == chunks + 2)
        def _():
            lax.fori_loop(0, subs, release, 0)

        @pl.when(t == chunks + 3)
        def _():
            dispatch_norm()

        @pl.when(t == chunks + 4)
        def _():
            relay_norm()

        stage(t, depth, expand)
        return carry

    lax.fori_loop(0, chunks + depth, forward, 0)

    def start_down(c, carry):
        down_copy(c).start()
        return carry

    lax.fori_loop(0, chunks, start_down, 0)
    settled(psend.at[pl.ds(0, heads - 1)], zs)
    settled(rrecv, pr.at[chunks])
    gate_scale = scale_ref[0, 0]
    up_scale = scale_ref[0, 1]
    down_scale = scale_ref[0, 2]

    def activate(i, carry):
        at = pl.ds(pl.multiple_of(i * slots, slots), slots)
        factor = jnp.sum(rrecv[i].astype(f32), axis=1, keepdims=True) / 64
        g = acc_g[at, :] * (factor * gate_scale)
        u = acc_u[at, :] * (factor * up_scale)
        act[at, :] = (g / (1.0 + jnp.exp(-g)) * u).astype(bf)
        return carry

    lax.fori_loop(0, seqs, activate, 0)

    def contract(c):
        @pl.when(c % 2 == 0)
        def _():
            down_copy(c // 2).wait()

        at = fcols(c)
        rows_out = jnp.dot(
            act[...],
            wbuf[c // 2, pl.ds(0, hidden), pl.ds(pl.multiple_of((c % 2) * fine, fine), fine)],
            preferred_element_type=f32,
        )
        recv[:, :, at] = (rows_out * down_scale).astype(bf).reshape(seqs, slots, fine)

        def give(o):
            for who in (1, 0) if woven else (0,):
                b1 = ways[o][0] if who else 0
                sem = (rl if who else rr).at[c]
                for n in range(count - 1, -1, -1):
                    d = lists[o][n]
                    src = recv.at[d ^ b1, :, at]
                    dst = back.at[who * count + n, :, at]
                    if d == 0:
                        pltpu.make_async_copy(src, dst, sem).start()
                    else:
                        remote(src, dst, rs, sem, flip(d), h).start()

        choose(c, give)

    def landing(c):
        return wbuf.at[
            c // 2,
            pl.ds(hidden, tokens),
            pl.ds(pl.multiple_of((c % 2) * fine, fine), fine),
        ]

    def unite(c):
        at = fcols(c)
        settled(back.at[pl.ds(count, count), :, at], rl.at[c])

        def work(o):
            total = jnp.dot(
                mix_ref[o, 1], back[pl.ds(count, count), :, at].reshape(owned, fine),
                preferred_element_type=f32,
            )
            nbr[:, at] = total.astype(bf)
            remote(
                nbr.at[:, at], landing(c), es, er.at[c], flip(ways[o][0]), h
            ).start()

        choose(c, work)

    def combine(c):
        at = fcols(c)
        settled(back.at[pl.ds(0, count), :, at], rr.at[c])
        if woven:
            settled(landing(c), er.at[c])

        def work(o):
            total = jnp.dot(
                mix_ref[o, 0], back[pl.ds(0, count), :, at].reshape(owned, fine),
                preferred_element_type=f32,
            )
            if woven:
                total = total + landing(c)[...].astype(f32)
            split_heads(total, at, fine)

        choose(c, work)
        for d in range(1, heads):
            remote(
                psend.at[line(d), :, at], precv.at[h, :, at], cs, cr.at[c], s, line(d)
            ).start()

    def finish(c):
        at = fcols(c)
        settled(precv.at[pl.ds(0, heads - 1), :, at], cr.at[c])
        total = res[:, at].astype(f32) + own[:, at]
        for d in range(1, heads):
            total = total + precv[line(d), :, at].astype(f32)
        out_ref[:, at] = total.astype(bf)

    lags = (0, 2, 4, 6) if woven else (0, 0, 3, 5)

    def backward(t, carry):
        for lag, work in zip(lags, (contract, unite, combine, finish)):
            if work is unite and not woven:
                continue

            @pl.when((t >= lag) & (t < pieces + lag))
            def _(lag=lag, work=work):
                work(t - lag)

        return carry

    lax.fori_loop(0, pieces + lags[-1], backward, 0)

    state_swap().wait_send()
    settled(pair_state.at[pl.ds(0, owners - 1), pl.ds(0, local // 2)], pair_s)
    settled(pair_state.at[pl.ds(0, owners - 1), pl.ds(0, local // 2)], fold_sem.at[0])
    settled(route.at[pl.ds(0, heads - 1)], route_sem.at[0])
    if relayed:

        @pl.when(inner)
        def _():
            settled(gath, gs.at[0])

        @pl.when(jnp.logical_not(inner))
        def _():
            settled(gath.at[band(0, 2), :], gs.at[0])
    else:
        settled(gath.at[band(0, heads - 1), :], gs.at[0])
    settled(rgath.at[band(0, heads - 1), :], gs.at[1])
    moved = seqs - 2 if woven else seqs - 1
    settled(send.at[pl.ds(0, moved)], ps.at[0])
    settled(rsend.at[pl.ds(0, moved)], ps.at[1])
    settled(recv.at[pl.ds(0, moved)], rs)
    settled(psend.at[pl.ds(0, heads - 1)], cs)
    if woven:
        settled(near_route, near_s)
        settled(nbr, ds.at[0])
        settled(rnbr, ds.at[1])
        settled(nbr, es)


def body(
    query,
    key,
    value,
    head_gain,
    out_weight,
    stream,
    model_gain,
    expert_ids,
    expert_gates,
    gate_weight,
    up_weight,
    down_weight,
    weight_scales,
):
    seqs, heads = lax.axis_size("seq"), lax.axis_size("head")
    tokens, features = query.shape
    rows, width = stream.shape
    hidden = gate_weight.shape[2]
    local = features // HD
    block = out_weight.shape[1]
    subs = block // SEG
    owners = seqs // 2
    chunks = 2 * subs
    step = owners * SEG
    woven = seqs == 8
    ways, sides = (2, 2) if woven else (1, 1)
    capacity = 3 * rows * TOPK // (2 * seqs * heads)
    slots = -(-capacity * heads // 16) * 16
    owned = (4 if woven else seqs) * slots
    deep = max(features, hidden + tokens if woven else hidden)
    vmem = pl.BlockSpec(memory_space=pltpu.VMEM)
    smem = pl.BlockSpec(memory_space=pltpu.SMEM)
    anywhere = pl.BlockSpec(memory_space=pl.ANY)
    bf, f32 = jnp.bfloat16, jnp.float32
    dma = pltpu.SemaphoreType.DMA
    return pl.pallas_call(
        functools.partial(layer_kernel, seqs, heads, slots),
        out_shape=jax.ShapeDtypeStruct((rows, width), bf),
        in_specs=[anywhere] * 3 + [vmem] + [anywhere] * 2 + [vmem] * 3 + [smem] + [anywhere] * 3,
        out_specs=vmem,
        scratch_shapes=[
            pltpu.VMEM((tokens, features), bf),
            pltpu.VMEM((tokens, features), bf),
            pltpu.VMEM((tokens, features), bf),
            pltpu.VMEM((rows, width), bf),
            pltpu.VMEM((2, local, HD, HD), bf),
            pltpu.VMEM((owners, local, HD, HD), bf),
            pltpu.VMEM((tokens, features), bf),
            pltpu.VMEM((chunks, deep, step), bf),
            pltpu.VMEM((heads, rows, step), f32),
            pltpu.VMEM((rows, width), f32),
            pltpu.VMEM((heads, rows, width), bf),
            pltpu.VMEM((heads, rows, width), bf),
            pltpu.VMEM((rows, width), bf),
            pltpu.VMEM((rows, SEG), f32),
            pltpu.VMEM((128, 128), f32),
            pltpu.VMEM((heads, 2 * TOPK, 128), f32),
            pltpu.VMEM((2, heads, 2 * TOPK, 128), f32),
            pltpu.VMEM((heads, rows, 128), f32),
            pltpu.VMEM((ways, sides, owned, tokens), bf),
            pltpu.VMEM((ways, sides, tokens, owned), bf),
            pltpu.VMEM((width, hidden), bf),
            pltpu.VMEM((width, hidden), bf),
            pltpu.VMEM((tokens, width), bf),
            pltpu.VMEM((tokens, width if woven else 128), bf),
            pltpu.VMEM((seqs, slots, width), bf),
            pltpu.VMEM((seqs, slots, width), bf),
            pltpu.VMEM((seqs, slots, width), bf),
            pltpu.VMEM((tokens, 128), bf),
            pltpu.VMEM((tokens, 128), bf),
            pltpu.VMEM((seqs, slots, 128), bf),
            pltpu.VMEM((seqs, slots, 128), bf),
            pltpu.VMEM((seqs * slots, hidden), f32),
            pltpu.VMEM((seqs * slots, hidden), f32),
            pltpu.VMEM((seqs * slots, hidden), bf),
            dma((2,)),
            dma,
            dma((owners,)),
            dma((2,)),
            dma((subs,)),
            dma((owners, subs, 2)),
            dma((subs,)),
            dma((subs,)),
            dma((2,)),
            dma,
            dma((2,)),
            dma,
            dma((chunks,)),
            dma((chunks,)),
            dma((2,)),
            dma((chunks + 1,)),
            dma((2,)),
            dma((chunks + 1,)),
            dma((2,)),
            dma((chunks + 1,)),
            dma,
            dma((2 * chunks,)),
            dma((2 * chunks,)),
            dma,
            dma((2 * chunks,)),
            dma,
            dma((2 * chunks,)),
            dma((4,)),
            dma((subs,)),
            dma((2, chunks)),
            dma((chunks,)),
        ],
        compiler_params=pltpu.CompilerParams(
            collective_id=0, has_side_effects=True, vmem_limit_bytes=67043328
        ),
    )(
        query,
        key,
        value,
        head_gain.reshape(1, -1),
        out_weight,
        stream,
        model_gain.reshape(1, -1),
        expert_ids.T,
        expert_gates.T,
        weight_scales,
        gate_weight,
        up_weight,
        down_weight,
    )


def solution(mesh):
    return jax.shard_map(
        body,
        mesh=mesh,
        in_specs=(
            P("seq", "head"),
            P("seq", "head"),
            P("seq", "head"),
            P("head"),
            P("head", "seq"),
            P(("seq", "head"), None),
            P(),
            P(("seq", "head"), None),
            P(("seq", "head"), None),
            P(("seq", "head"), None, None),
            P(("seq", "head"), None, None),
            P(("seq", "head"), None, None),
            P(("seq", "head"), None),
        ),
        out_specs=P(("seq", "head"), None),
        check_vma=False,
    )
```
